32 devices in a mesh: dp: 2 (over x), expert: 16 (over z, y, core).
Axes of the slice: x: 2, y: 2, z: 4, core: 2. Of those that a mesh axis runs over, the one named last changes fastest.
Arguments:
- tokens: bfloat16 [4096, 2048], P(('dp', 'expert')), may hold values from -6 to 6
- cotangent: bfloat16 [4096, 2048], P(('dp', 'expert')), may hold values from -6 to 6
- expert_ids: int32 [4096, 8], P(('dp', 'expert')), may hold values from 0 to 127, as said below
- gate_probs: float32 [4096, 8], P(('dp', 'expert')), may hold values from 0.1 to 1
- gate_weight: bfloat16 [16, 2048, 128], P('expert'), may hold values from -0.125 to 0.125
- up_weight: bfloat16 [16, 2048, 128], P('expert'), may hold values from -0.125 to 0.125
- down_weight: bfloat16 [16, 128, 2048], P('expert'), may hold values from -0.1875 to 0.1875
Outputs:
- grad_input: bfloat16 [4096, 2048], P(('dp', 'expert'))
- grad_gate: bfloat16 [16, 2048, 128], P('expert')
- grad_up: bfloat16 [16, 2048, 128], P('expert')
- grad_down: bfloat16 [16, 128, 2048], P('expert')
The draws below stay inside these ranges and needn't reach their ends.
Inputs may be any that keep to these rules, and one draw needn't show every extreme that they name: `expert_ids`: each row names 8 different experts. Among the 128 rows of one device, each window expert 0 to 1 is named by 1 to 8 rows, and in every draw one window expert of every device is named by exactly 8 rows.
All inputs are finite; a program needn't handle non-finite values.
Results may differ from the reference program's by a relative error of at most 0.0064.
Values may be sent and summed in bfloat16 or wider, within the bound.
No kernel may reach another device: no remote copies, remote signals or barrier semaphores. Data moves between devices by JAX's collectives and lax.ppermute only.
A program may use at most 64 MiB of HBM per device.

```python
import math
import jax
import jax.numpy as jnp
from jax import lax

D = 2048
HID = 1024
EXPERTS = 128
TOP = 8
SLICES = 8
TOK_DEV = 128
CAP = 8
HSL = 128
EXP_WIN = 2
TOKENS = 4096


def draw_expert_ids(key, part):
    blocks = TOKENS // TOK_DEV
    window = EXP_WIN
    others = EXPERTS - window
    key_count, key_full, key_member, key_other, key_order = jax.random.split(jax.random.fold_in(key, 17), 5)
    counts = jax.random.randint(key_count, (blocks, window), 1, CAP + 1)
    full_one = jax.random.randint(key_full, (blocks,), 0, window)
    counts = jnp.where(jnp.arange(window)[None, :] == full_one[:, None], CAP, counts)
    member_score = jax.random.randint(key_member, (blocks, window, TOK_DEV), 0, 1 << 20) * TOK_DEV + jnp.arange(TOK_DEV)
    ordering = jnp.argsort(member_score, axis=-1)
    ranking = jnp.argsort(ordering, axis=-1)
    member = jnp.transpose(ranking < counts[:, :, None], (0, 2, 1)).astype(jnp.int32)
    window_key = (1 - member) * window + jnp.arange(window)
    window_sorted = jnp.argsort(window_key, axis=-1)
    window_count = jnp.sum(member, axis=-1)
    other_score = jax.random.randint(key_other, (blocks, TOK_DEV, others), 0, 1 << 20) * others + jnp.arange(others)
    unused, other_top = lax.top_k(other_score, TOP)
    other_ids = other_top + window
    position = jnp.arange(TOP)[None, None, :]
    window_pick = jnp.take_along_axis(window_sorted, jnp.broadcast_to(jnp.minimum(position, window - 1), (blocks, TOK_DEV, TOP)), axis=-1)
    other_index = jnp.clip(position - window_count[..., None], 0, TOP - 1)
    other_pick = jnp.take_along_axis(other_ids, other_index, axis=-1)
    combined = jnp.where(position < window_count[..., None], window_pick, other_pick)
    shuffle_score = jax.random.randint(key_order, (blocks, TOK_DEV, TOP), 0, 1 << 20) * TOP + position
    shuffle = jnp.argsort(shuffle_score, axis=-1)
    combined = jnp.take_along_axis(combined, shuffle, axis=-1)
    return combined.reshape(TOKENS, TOP).astype(jnp.int32)


def levels(rng, extent, cuts, low, high):
    gain = 1.0
    for dim, shards_of in cuts:
        draws = jax.random.uniform(jax.random.fold_in(jax.random.fold_in(rng, 6), dim), (shards_of,), jnp.float32, low / len(cuts), high / len(cuts))
        gain = gain * jnp.repeat(jnp.exp(draws), extent[dim] // shards_of).reshape((-1,) + (1,) * (len(extent) - 1 - dim))
    return gain


def gaussian(rng, dims, spread, reach, shards=(), kind=jnp.bfloat16):
    loudness = levels(rng, dims, shards, -0.22, 0.18) if shards else 1.0
    entries = jax.random.normal(rng, dims, jnp.float32) * spread * loudness
    return jnp.minimum(jnp.maximum(entries, -reach), reach).astype(kind)


def setup_inputs(seed: int = 0) -> dict:
    splits = jax.random.split(jax.random.key(seed), 8)
    return {
        "tokens": gaussian(splits[0], (TOKENS, D), 1.0, 6.0, ((0, 32),)),
        "cotangent": gaussian(splits[1], (TOKENS, D), 1.0, 6.0, ((0, 32),)),
        "expert_ids": draw_expert_ids(jax.random.fold_in(splits[7], 71), 0),
        "gate_probs": jnp.clip(jnp.exp(math.log(1.0) - 2.3025851 * jax.random.uniform(splits[3], (TOKENS, TOP), jnp.float32) ** levels(splits[3], (TOKENS, TOP), ((0, 32),), -0.2, 0.2)), 0.1, 1.0),
        "gate_weight": gaussian(splits[4], (SLICES * EXP_WIN, D, HSL), D ** -0.5, 0.125, ((0, 16),)),
        "up_weight": gaussian(splits[5], (SLICES * EXP_WIN, D, HSL), D ** -0.5, 0.125, ((0, 16),)),
        "down_weight": gaussian(splits[6], (SLICES * EXP_WIN, HSL, D), HID ** -0.5, 0.1875, ((0, 16),)),
    }


def silu_parts(gate_pre):
    sigmoid_value = jax.nn.sigmoid(gate_pre)
    return gate_pre * sigmoid_value, sigmoid_value * (1.0 + gate_pre * (1.0 - sigmoid_value))


def expert_slice(rows_in, rows_cot, gate_rows, up_rows, down_rows):
    gate_pre = jnp.dot(rows_in, gate_rows, preferred_element_type=jnp.float32)
    upward = jnp.dot(rows_in, up_rows, preferred_element_type=jnp.float32)
    swish, slope = silu_parts(gate_pre)
    active = (swish * upward).astype(jnp.bfloat16)
    dhidden = lax.dot_general(rows_cot, down_rows, (((1,), (1,)), ((), ())), preferred_element_type=jnp.float32)
    dgate = (dhidden * upward * slope).astype(jnp.bfloat16)
    dupward = (dhidden * swish).astype(jnp.bfloat16)
    grad_down = lax.dot_general(active, rows_cot, (((0,), (0,)), ((), ())), preferred_element_type=jnp.float32)
    grad_gate = lax.dot_general(rows_in, dgate, (((0,), (0,)), ((), ())), preferred_element_type=jnp.float32)
    grad_up = lax.dot_general(rows_in, dupward, (((0,), (0,)), ((), ())), preferred_element_type=jnp.float32)
    partial_value = lax.dot_general(dgate, gate_rows, (((1,), (1,)), ((), ())), preferred_element_type=jnp.float32)
    partial_value = partial_value + lax.dot_general(dupward, up_rows, (((1,), (1,)), ((), ())), preferred_element_type=jnp.float32)
    return partial_value, grad_gate, grad_up, grad_down


def reference(tokens, cotangent, expert_ids, gate_probs, gate_weight, up_weight, down_weight):
    blocks = TOKENS // TOK_DEV
    window = EXP_WIN
    id_blocks = expert_ids.reshape(blocks, TOK_DEV, TOP)
    prob_blocks = gate_probs.reshape(blocks, TOK_DEV, TOP)
    matched = id_blocks[..., None] == jnp.arange(window, dtype=jnp.int32)
    hit_count = jnp.sum(matched.astype(jnp.int32), axis=2)
    chosen = jnp.sum(jnp.where(matched, prob_blocks[..., None], jnp.float32(0)), axis=2)
    slot_rank = jnp.cumsum(hit_count, axis=1) - hit_count
    placed = (hit_count[..., None] == 1) & (slot_rank[..., None] == jnp.arange(CAP, dtype=jnp.int32))
    filled = jnp.any(placed, axis=1)
    positions = jnp.arange(TOK_DEV, dtype=jnp.int32)[None, :, None, None]
    owner_row = jnp.sum(jnp.where(placed, positions, 0), axis=1).astype(jnp.int32)
    block_index = jnp.arange(blocks, dtype=jnp.int32)[:, None, None]
    tok_blocks = tokens.reshape(blocks, TOK_DEV, D)
    cot_blocks = cotangent.reshape(blocks, TOK_DEV, D)
    rows_in = jnp.where(filled[..., None], tok_blocks[block_index, owner_row], jnp.zeros((), tokens.dtype))
    slot_prob = jnp.take_along_axis(jnp.transpose(chosen, (0, 2, 1)), owner_row, axis=2)
    scaled = slot_prob[..., None] * cot_blocks[block_index, owner_row].astype(jnp.float32)
    rows_cot = jnp.where(filled[..., None], scaled, jnp.float32(0)).astype(jnp.bfloat16)
    gate_list = []
    up_list = []
    down_list = []
    back_list = [jnp.zeros((blocks * CAP, D), jnp.float32) for expert_index in range(window)]
    for slice_index in range(SLICES):
        for expert_index in range(window):
            weight_row = slice_index * window + expert_index
            expert_in = rows_in[:, expert_index].reshape(blocks * CAP, D)
            expert_cot = rows_cot[:, expert_index].reshape(blocks * CAP, D)
            partial_value, grad_g, grad_u, grad_d = expert_slice(expert_in, expert_cot, gate_weight[weight_row], up_weight[weight_row], down_weight[weight_row])
            rounded = lax.optimization_barrier(partial_value.astype(jnp.bfloat16)).astype(jnp.float32)
            back_list[expert_index] = back_list[expert_index] + rounded
            gate_list.append(grad_g.astype(jnp.bfloat16))
            up_list.append(grad_u.astype(jnp.bfloat16))
            down_list.append(grad_d.astype(jnp.bfloat16))
    back_all = jnp.stack([item.reshape(blocks, CAP, D) for item in back_list], axis=1)
    grad_blocks = jnp.zeros((blocks, TOK_DEV, D), jnp.float32)
    grad_blocks = grad_blocks.at[block_index, owner_row].add(jnp.where(filled[..., None], back_all, jnp.float32(0)))
    grad_input = grad_blocks.reshape(TOKENS, D).astype(jnp.bfloat16)
    return grad_input, jnp.stack(gate_list), jnp.stack(up_list), jnp.stack(down_list)
```

```python
import jax
import jax.numpy as jnp
from jax import lax
from jax.sharding import PartitionSpec as P

SLICES = 8
CAP = 8
MASKS = (1, 2, 6)


def silu_parts(gate_pre):
    sigmoid_value = jax.nn.sigmoid(gate_pre)
    return (gate_pre * sigmoid_value, sigmoid_value * (1.0 + gate_pre * (1.0 - sigmoid_value)))


def hidden(rows, gate_rows, up_rows, down_rows):
    width = gate_rows.shape[0]
    rows_in, rows_cot = rows[:, :width], rows[:, width:]
    gate_pre = jnp.dot(rows_in, gate_rows, preferred_element_type=jnp.float32)
    upward = jnp.dot(rows_in, up_rows, preferred_element_type=jnp.float32)
    dhidden = lax.dot_general(
        rows_cot, down_rows, (((1,), (1,)), ((), ())), preferred_element_type=jnp.float32
    )
    swish, slope = silu_parts(gate_pre)
    active = (swish * upward).astype(jnp.bfloat16)
    dgate = (dhidden * upward * slope).astype(jnp.bfloat16)
    dupward = (dhidden * swish).astype(jnp.bfloat16)
    return active, dgate, dupward


def part_of(dgate, dupward, gate_rows, up_rows):
    dims = (((1,), (1,)), ((), ()))
    value = lax.dot_general(dgate, gate_rows, dims, preferred_element_type=jnp.float32)
    return value + lax.dot_general(dupward, up_rows, dims, preferred_element_type=jnp.float32)


def weight_grads(rows, hid):
    active, dgate, dupward = hid
    width = rows.shape[1] // 2
    rows_in, rows_cot = rows[:, :width], rows[:, width:]
    dims = (((0,), (0,)), ((), ()))
    return (
        lax.dot_general(rows_in, dgate, dims, preferred_element_type=jnp.float32),
        lax.dot_general(rows_in, dupward, dims, preferred_element_type=jnp.float32),
        lax.dot_general(active, rows_cot, dims, preferred_element_type=jnp.float32),
    )


def local(tokens, cotangent, expert_ids, gate_probs, gate_weight, up_weight, down_weight):
    devices = lax.axis_size("expert")
    groups = lax.axis_size("dp")
    window = devices // SLICES
    width = tokens.shape[1]
    mine = lax.rem(lax.axis_index("expert"), window)
    gate_rows, up_rows, down_rows = gate_weight[0], up_weight[0], down_weight[0]

    def swap_expert(value, bit):
        pairs = [(i, i ^ bit) for i in range(devices)]
        return lax.ppermute(value, "expert", pairs)

    def swap_slice(value, stage):
        pairs = []
        for i in range(devices):
            mask = MASKS[(stage + i % window) % len(MASKS)]
            pairs.append((i, i ^ (mask * window)))
        return lax.ppermute(value, "expert", pairs)

    def swap_dp(value, mask):
        return lax.ppermute(value, "dp", [(i, i ^ mask) for i in range(groups)])

    experts = mine ^ jnp.arange(window, dtype=jnp.int32)
    matched = expert_ids[:, :, None] == experts[None, None, :]
    hit_count = jnp.sum(matched.astype(jnp.int32), axis=1)
    chosen = jnp.sum(jnp.where(matched, gate_probs[:, :, None], 0.0), axis=1)
    slot_rank = jnp.cumsum(hit_count, axis=0) - hit_count
    placed = (hit_count[:, :, None] == 1) & (
        slot_rank[:, :, None] == jnp.arange(CAP, dtype=jnp.int32)[None, None, :]
    )
    picker = placed.astype(jnp.bfloat16)
    slot_prob = jnp.sum(jnp.where(placed, chosen[:, :, None], 0.0), axis=0)
    rows_in = jnp.einsum("tec,td->ecd", picker, tokens, preferred_element_type=jnp.float32)
    picked_cot = jnp.einsum("tec,td->ecd", picker, cotangent, preferred_element_type=jnp.float32)
    rows = jnp.concatenate(
        [rows_in.astype(jnp.bfloat16), (slot_prob[:, :, None] * picked_cot).astype(jnp.bfloat16)],
        axis=2,
    )

    bit = window // 2
    while bit:
        received = swap_expert(rows[bit:], bit)
        rows = jnp.concatenate([rows[:bit], received], axis=1)
        bit //= 2
    held = rows[0]

    pieces = [held]
    for stage in range(len(MASKS)):
        received = swap_slice(held, stage)
        pieces.append(received)
        held = jnp.concatenate([held, received], axis=0)

    own_hidden = [hidden(piece, gate_rows, up_rows, down_rows) for piece in pieces]
    parts = [part_of(h[1], h[2], gate_rows, up_rows) for h in own_hidden]

    for stage in reversed(range(len(MASKS))):
        received = swap_slice(parts[stage + 1].astype(jnp.bfloat16), stage)
        offset = 0
        for index in range(stage + 1):
            size = parts[index].shape[0]
            parts[index] = parts[index] + received[offset : offset + size].astype(jnp.float32)
            offset += size
    back = parts[0].astype(jnp.bfloat16)[None]
    bit = 1
    while bit < window:
        half = back.shape[1] // 2
        received = swap_expert(back[:, half:], bit)
        back = jnp.concatenate([back[:, :half], received], axis=0)
        bit *= 2
    grad_input = jnp.einsum("tec,ecd->td", picker, back, preferred_element_type=jnp.float32).astype(
        jnp.bfloat16
    )

    joined = [jnp.concatenate(items, axis=0) for items in zip(*own_hidden)]
    grads = weight_grads(held, joined)
    for mask in range(1, groups):
        theirs = [swap_dp(item, mask) for item in (jnp.concatenate(pieces[:2]), pieces[2], pieces[3])]
        their_hidden = [hidden(piece, gate_rows, up_rows, down_rows) for piece in theirs]
        joined = [jnp.concatenate(items, axis=0) for items in zip(*their_hidden)]
        more = weight_grads(jnp.concatenate(theirs, axis=0), joined)
        grads = tuple(a + b for a, b in zip(grads, more))
    return (grad_input,) + tuple(g.astype(jnp.bfloat16)[None] for g in grads)


def solution(mesh):
    rows = P(("dp", "expert"), None)
    weight = P("expert", None, None)
    return jax.shard_map(
        local,
        mesh=mesh,
        in_specs=(rows, rows, rows, rows, weight, weight, weight),
        out_specs=(rows, weight, weight, weight),
        check_vma=False,
    )
```

```python
import functools

import jax
import jax.numpy as jnp
from jax import lax
from jax.experimental import pallas as pl
from jax.experimental.pallas import tpu as pltpu
from jax.sharding import Mesh, PartitionSpec as P


SLICES = 8
CAP = 8
FAR = 4


NT = (((1,), (1,)), ((), ()))
TN = (((0,), (0,)), ((), ()))


def silu_parts(gate_pre):
    sigmoid_value = jax.nn.sigmoid(gate_pre)
    return (gate_pre * sigmoid_value, sigmoid_value * (1.0 + gate_pre * (1.0 - sigmoid_value)))


def hidden(rows, gate_rows, up_rows, down_rows):
    width = gate_rows.shape[0]
    rows_in, rows_cot = rows[:, :width], rows[:, width:]
    gate_pre = jnp.dot(rows_in, gate_rows, preferred_element_type=jnp.float32)
    upward = jnp.dot(rows_in, up_rows, preferred_element_type=jnp.float32)
    dhidden = lax.dot_general(rows_cot, down_rows, NT, preferred_element_type=jnp.float32)
    swish, slope = silu_parts(gate_pre)
    active = (swish * upward).astype(jnp.bfloat16)
    dgate = (dhidden * upward * slope).astype(jnp.bfloat16)
    dupward = (dhidden * swish).astype(jnp.bfloat16)
    return active, dgate, dupward


def part_of(hid, gate_rows, up_rows):
    value = lax.dot_general(hid[1], gate_rows, NT, preferred_element_type=jnp.float32)
    return value + lax.dot_general(hid[2], up_rows, NT, preferred_element_type=jnp.float32)


def weight_grads(rows, hid):
    active, dgate, dupward = hid
    width = rows.shape[1] // 2
    rows_in, rows_cot = rows[:, :width], rows[:, width:]
    return (
        lax.dot_general(rows_in, dgate, TN, preferred_element_type=jnp.float32),
        lax.dot_general(rows_in, dupward, TN, preferred_element_type=jnp.float32),
        lax.dot_general(active, rows_cot, TN, preferred_element_type=jnp.float32),
    )


def front_kernel(window, mine_ref, ids_hbm, probs_hbm, tokens_hbm, cot_hbm, rows_ref, picker_ref,
                 ids_ref, probs_ref, tokens_ref, cot_ref, sems):
    copies = [
        pltpu.make_async_copy(source, target, sems.at[index])
        for index, (source, target) in enumerate(
            (
                (ids_hbm, ids_ref),
                (probs_hbm, probs_ref),
                (tokens_hbm, tokens_ref),
                (cot_hbm, cot_ref),
            )
        )
    ]
    for copy in copies:
        copy.start()
    mine = mine_ref[0]
    count, width = tokens_ref.shape
    slots = window * CAP
    slot = lax.broadcasted_iota(jnp.int32, (slots, count), 0)
    earlier = lax.broadcasted_iota(jnp.int32, (count, count), 0) < lax.broadcasted_iota(
        jnp.int32, (count, count), 1
    )
    copies[0].wait()
    copies[1].wait()
    ids = ids_ref[...]
    probs = probs_ref[...]
    hit = jnp.zeros((slots, count), jnp.float32)
    chosen = jnp.zeros((slots, count), jnp.float32)
    for index in range(window):
        match = ids == (mine ^ index)
        hits = jnp.sum(match.astype(jnp.float32), axis=0, keepdims=True)
        prob = jnp.sum(jnp.where(match, probs, 0.0), axis=0, keepdims=True)
        here = slot // CAP == index
        hit = jnp.where(here, hits, hit)
        chosen = jnp.where(here, prob, chosen)
    rank = jnp.dot(
        hit.astype(jnp.bfloat16), earlier.astype(jnp.bfloat16), preferred_element_type=jnp.float32
    )
    placed = (hit == 1.0) & (rank.astype(jnp.int32) == slot % CAP)
    picker = placed.astype(jnp.bfloat16)
    picker_ref[...] = picker
    prob = jnp.sum(jnp.where(placed, chosen, 0.0), axis=1, keepdims=True)
    copies[2].wait()
    rows_in = jnp.dot(picker, tokens_ref[...], preferred_element_type=jnp.float32)
    rows_ref[:, :width] = rows_in.astype(jnp.bfloat16)
    copies[3].wait()
    rows_cot = jnp.dot(picker, cot_ref[...], preferred_element_type=jnp.float32)
    rows_ref[:, width:] = (prob * rows_cot).astype(jnp.bfloat16)


def front(mine, ids, probs, tokens, cotangent, window):
    count, width = tokens.shape
    slots = window * CAP
    vmem = pl.BlockSpec(memory_space=pltpu.VMEM)
    away = pl.BlockSpec(memory_space=pltpu.HBM)
    return pl.pallas_call(
        functools.partial(front_kernel, window),
        out_shape=(
            jax.ShapeDtypeStruct((slots, 2 * width), jnp.bfloat16),
            jax.ShapeDtypeStruct((slots, count), jnp.bfloat16),
        ),
        in_specs=[pl.BlockSpec(memory_space=pltpu.SMEM), away, away, away, away],
        out_specs=(vmem, vmem),
        scratch_shapes=[
            pltpu.VMEM(ids.shape, ids.dtype),
            pltpu.VMEM(probs.shape, probs.dtype),
            pltpu.VMEM(tokens.shape, tokens.dtype),
            pltpu.VMEM(cotangent.shape, cotangent.dtype),
            pltpu.SemaphoreType.DMA((4,)),
        ],
        compiler_params=pltpu.CompilerParams(vmem_limit_bytes=8 << 20),
        name="front",
    )(mine, ids, probs, tokens, cotangent)


TILES = 8


def finish_kernel(gate_ref, up_ref, down_ref, rows_ref, active_ref, dgate_ref, dupward_ref,
                  gate_hbm, up_hbm, down_hbm, gate_out, up_out, down_out, sems):
    width = gate_ref.shape[0]
    tile = width // TILES
    copies = []

    def send(source, target, index):
        copy = pltpu.make_async_copy(source, target, sems.at[index])
        copy.start()
        copies.append(copy)

    for index in range(TILES):
        part = pl.ds(index * tile, tile)
        rows_in = rows_ref[:, index * tile : (index + 1) * tile]
        rows_cot = rows_ref[:, width + index * tile : width + (index + 1) * tile]
        for source, slope, out, hbm, sem in (
            (gate_ref, dgate_ref, gate_out, gate_hbm, 0),
            (up_ref, dupward_ref, up_out, up_hbm, 1),
        ):
            more = lax.dot_general(rows_in, slope[...], TN, preferred_element_type=jnp.float32)
            out[part, :] = (source[part, :] + more).astype(jnp.bfloat16)
            send(out.at[part, :], hbm.at[part, :], 3 * index + sem)
        more = lax.dot_general(active_ref[...], rows_cot, TN, preferred_element_type=jnp.float32)
        down_out[:, part] = (down_ref[:, part] + more).astype(jnp.bfloat16)
        send(down_out.at[:, part], down_hbm.at[:, part], 3 * index + 2)
    for copy in copies:
        copy.wait()


def finish(grads, rows, hid):
    vmem = pl.BlockSpec(memory_space=pltpu.VMEM)
    away = pl.BlockSpec(memory_space=pltpu.HBM)
    return pl.pallas_call(
        finish_kernel,
        out_shape=tuple(jax.ShapeDtypeStruct(g.shape, jnp.bfloat16) for g in grads),
        in_specs=[vmem] * 7,
        out_specs=(away,) * 3,
        scratch_shapes=[pltpu.VMEM(g.shape, jnp.bfloat16) for g in grads]
        + [pltpu.SemaphoreType.DMA((3 * TILES,))],
        compiler_params=pltpu.CompilerParams(vmem_limit_bytes=12 << 20),
        name="finish",
    )(*grads, rows, *hid)


def local(tokens, cotangent, expert_ids, gate_probs, gate_weight, up_weight, down_weight):
    groups = lax.axis_size("dp")
    window = lax.axis_size("win")
    mine = lax.axis_index("win")
    weights = (gate_weight[0], up_weight[0], down_weight[0])
    block = window * CAP

    def swap(value, axis, mask):
        pairs = [(i, i ^ mask) for i in range(lax.axis_size(axis))]
        return lax.ppermute(value, axis, pairs)

    def join(items):
        return jnp.concatenate(items, axis=0)

    rows, picker = front(
        mine.astype(jnp.int32)[None], expert_ids.T, gate_probs.T, tokens, cotangent, window
    )
    held = [rows[:CAP]]
    for index in range(1, window):
        held.append(swap(rows[index * CAP : (index + 1) * CAP], "win", index))

    rows = {0: join(held)}
    for mask in (6, 4, 2):
        rows[mask] = swap(rows[0], "slice", mask)
    for mask in (0, 2, 6, 4):
        rows[mask + 1] = swap(rows[mask], "slice", 1)

    def pair(mask):
        return join([rows[mask], rows[mask ^ FAR]])

    even = join([pair(0), pair(2)])
    hid_even = hidden(even, *weights)
    part = part_of(hid_even, *weights[:2])
    back = part[: 2 * block]
    part = part[2 * block :].astype(jnp.bfloat16)
    incoming = [swap(part, "slice", 2)]
    piece, _ = lax.optimization_barrier((pair(3), part))
    hid_three = hidden(piece, *weights)
    part = part_of(hid_three, *weights[:2]).astype(jnp.bfloat16)
    incoming.append(swap(part, "slice", 3))
    piece, _ = lax.optimization_barrier((pair(1), part))
    hid_one = hidden(piece, *weights)
    part = part_of(hid_one, *weights[:2]).astype(jnp.bfloat16)
    incoming.append(swap(part, "slice", 1))
    last = part
    for part in incoming:
        back = back + part.astype(jnp.float32)

    far = swap(back[block:].astype(jnp.bfloat16), "slice", FAR)
    back = (back[:block] + far.astype(jnp.float32)).astype(jnp.bfloat16)
    kept = [back[:CAP]]
    for index in range(1, window):
        kept.append(swap(back[index * CAP : (index + 1) * CAP], "win", index))
    grad_input = lax.dot_general(
        picker, join(kept), TN, preferred_element_type=jnp.float32
    ).astype(jnp.bfloat16)

    hid = [join(items) for items in zip(hid_even, hid_three, hid_one)]
    grads = weight_grads(join([even, pair(3), pair(1)]), hid)
    grads = lax.optimization_barrier(grads)
    for mask in range(1, groups):
        pieces = [rows[0], join([rows[2], rows[4], rows[6]]), pair(3), pair(1)]
        if mask > 1:
            pieces, grads = lax.optimization_barrier((pieces, grads))
        theirs = [swap(piece, "dp", mask) for piece in pieces]
        early, _ = lax.optimization_barrier((theirs[:-1], last))
        early = join(early)
        more = weight_grads(early, hidden(early, *weights))
        grads = tuple(a + b for a, b in zip(grads, more))
        late, _ = lax.optimization_barrier((theirs[-1], grad_input))
        hid = hidden(late, *weights)
        if mask < groups - 1:
            more = weight_grads(late, hid)
            grads = tuple(a + b for a, b in zip(grads, more))
    grads = finish(grads, late, hid)
    return (grad_input,) + tuple(g[None] for g in grads)


def solution(mesh):
    groups, devices = mesh.shape["dp"], mesh.shape["expert"]
    shape = (groups, SLICES, devices // SLICES)
    fine = Mesh(mesh.devices.reshape(shape), ("dp", "slice", "win"))
    rows = P(("dp", "slice", "win"), None)
    weight = P(("slice", "win"), None, None)
    return jax.shard_map(
        local,
        mesh=fine,
        in_specs=(rows, rows, rows, rows, weight, weight, weight),
        out_specs=(rows, weight, weight, weight),
        check_vma=False,
    )
```

```python
import functools

import jax
import jax.numpy as jnp
from jax import lax
from jax.experimental import pallas as pl
from jax.experimental.pallas import tpu as pltpu
from jax.sharding import Mesh, PartitionSpec as P


SLICES = 8
CAP = 8
FAR = 4


FRONT_VMEM = 55000 << 10
CHUNKS = 4

NT = (((1,), (1,)), ((), ()))
TN = (((0,), (0,)), ((), ()))


def silu_parts(gate_pre):
    sigmoid_value = jax.nn.sigmoid(gate_pre)
    return (gate_pre * sigmoid_value, sigmoid_value * (1.0 + gate_pre * (1.0 - sigmoid_value)))


def hidden(rows, gate_rows, up_rows, down_rows):
    width = gate_rows.shape[0]
    rows_in, rows_cot = rows[:, :width], rows[:, width:]
    gate_pre = jnp.dot(rows_in, gate_rows, preferred_element_type=jnp.float32)
    upward = jnp.dot(rows_in, up_rows, preferred_element_type=jnp.float32)
    dhidden = lax.dot_general(rows_cot, down_rows, NT, preferred_element_type=jnp.float32)
    swish, slope = silu_parts(gate_pre)
    active = (swish * upward).astype(jnp.bfloat16)
    dgate = (dhidden * upward * slope).astype(jnp.bfloat16)
    dupward = (dhidden * swish).astype(jnp.bfloat16)
    return active, dgate, dupward


def part_of(hid, gate_rows, up_rows):
    value = lax.dot_general(hid[1], gate_rows, NT, preferred_element_type=jnp.float32)
    return value + lax.dot_general(hid[2], up_rows, NT, preferred_element_type=jnp.float32)


def weight_grads(rows, hid):
    active, dgate, dupward = hid
    width = rows.shape[1] // 2
    rows_in, rows_cot = rows[:, :width], rows[:, width:]
    return (
        lax.dot_general(rows_in, dgate, TN, preferred_element_type=jnp.float32),
        lax.dot_general(rows_in, dupward, TN, preferred_element_type=jnp.float32),
        lax.dot_general(active, rows_cot, TN, preferred_element_type=jnp.float32),
    )


def front_kernel(window, mine_ref, ids_hbm, probs_hbm, tokens_hbm, cot_hbm, rows_ref, picker_ref,
                 ids_ref, probs_ref, tokens_ref, cot_ref, sems):
    copies = [
        pltpu.make_async_copy(ids_hbm, ids_ref, sems.at[0]),
        pltpu.make_async_copy(probs_hbm, probs_ref, sems.at[1]),
    ]
    size = tokens_ref.shape[0] // CHUNKS
    for source, target in ((tokens_hbm, tokens_ref), (cot_hbm, cot_ref)):
        for index in range(CHUNKS):
            part = pl.ds(index * size, size)
            copies.append(
                pltpu.make_async_copy(source.at[part], target.at[part], sems.at[len(copies)])
            )
    for copy in copies:
        copy.start()
    mine = mine_ref[0]
    count, width = tokens_ref.shape
    slots = window * CAP
    slot = lax.broadcasted_iota(jnp.int32, (slots, count), 0)
    earlier = lax.broadcasted_iota(jnp.int32, (count, count), 0) < lax.broadcasted_iota(
        jnp.int32, (count, count), 1
    )
    copies[0].wait()
    copies[1].wait()
    ids = ids_ref[...]
    probs = probs_ref[...]
    hit = jnp.zeros((slots, count), jnp.float32)
    chosen = jnp.zeros((slots, count), jnp.float32)
    for index in range(window):
        match = ids == (mine ^ index)
        hits = jnp.sum(match.astype(jnp.float32), axis=0, keepdims=True)
        prob = jnp.sum(jnp.where(match, probs, 0.0), axis=0, keepdims=True)
        here = slot // CAP == index
        hit = jnp.where(here, hits, hit)
        chosen = jnp.where(here, prob, chosen)
    rank = jnp.dot(
        hit.astype(jnp.bfloat16), earlier.astype(jnp.bfloat16), preferred_element_type=jnp.float32
    )
    placed = (hit == 1.0) & (rank.astype(jnp.int32) == slot % CAP)
    picker = placed.astype(jnp.bfloat16)
    picker_ref[...] = picker
    prob = jnp.sum(jnp.where(placed, chosen, 0.0), axis=1, keepdims=True)
    for copy in copies[2 : 2 + CHUNKS]:
        copy.wait()
    rows_in = jnp.dot(picker, tokens_ref[...], preferred_element_type=jnp.float32)
    rows_ref[:, :width] = rows_in.astype(jnp.bfloat16)
    for copy in copies[2 + CHUNKS :]:
        copy.wait()
    rows_cot = jnp.dot(picker, cot_ref[...], preferred_element_type=jnp.float32)
    rows_ref[:, width:] = (prob * rows_cot).astype(jnp.bfloat16)


def front(mine, ids, probs, tokens, cotangent, window):
    count, width = tokens.shape
    slots = window * CAP
    vmem = pl.BlockSpec(memory_space=pltpu.VMEM)
    away = pl.BlockSpec(memory_space=pltpu.HBM)
    return pl.pallas_call(
        functools.partial(front_kernel, window),
        out_shape=(
            jax.ShapeDtypeStruct((slots, 2 * width), jnp.bfloat16),
            jax.ShapeDtypeStruct((slots, count), jnp.bfloat16),
        ),
        in_specs=[pl.BlockSpec(memory_space=pltpu.SMEM), away, away, away, away],
        out_specs=(vmem, vmem),
        scratch_shapes=[
            pltpu.VMEM(ids.shape, ids.dtype),
            pltpu.VMEM(probs.shape, probs.dtype),
            pltpu.VMEM(tokens.shape, tokens.dtype),
            pltpu.VMEM(cotangent.shape, cotangent.dtype),
            pltpu.SemaphoreType.DMA((2 + 2 * CHUNKS,)),
        ],
        compiler_params=pltpu.CompilerParams(vmem_limit_bytes=FRONT_VMEM),
        name="front",
    )(mine, ids, probs, tokens, cotangent)


TILES = 8


def finish_kernel(gate_ref, up_ref, down_ref, rows_ref, active_ref, dgate_ref, dupward_ref,
                  gate_hbm, up_hbm, down_hbm, gate_out, up_out, down_out, sems):
    width = gate_ref.shape[0]
    tile = width // TILES
    copies = []

    def send(source, target, index):
        copy = pltpu.make_async_copy(source, target, sems.at[index])
        copy.start()
        copies.append(copy)

    units = dgate_ref.shape[1]
    slopes = jnp.concatenate([dgate_ref[...], dupward_ref[...]], axis=1)
    for index in range(TILES):
        part = pl.ds(index * tile, tile)
        rows_in = rows_ref[:, index * tile : (index + 1) * tile]
        rows_cot = rows_ref[:, width + index * tile : width + (index + 1) * tile]
        both = lax.dot_general(rows_in, slopes, TN, preferred_element_type=jnp.float32)
        for source, more, out, hbm, sem in (
            (gate_ref, both[:, :units], gate_out, gate_hbm, 0),
            (up_ref, both[:, units:], up_out, up_hbm, 1),
        ):
            out[part, :] = (source[part, :] + more).astype(jnp.bfloat16)
            send(out.at[part, :], hbm.at[part, :], 3 * index + sem)
        more = lax.dot_general(active_ref[...], rows_cot, TN, preferred_element_type=jnp.float32)
        down_out[:, part] = (down_ref[:, part] + more).astype(jnp.bfloat16)
        send(down_out.at[:, part], down_hbm.at[:, part], 3 * index + 2)
    for copy in copies:
        copy.wait()


def finish(grads, rows, hid):
    vmem = pl.BlockSpec(memory_space=pltpu.VMEM)
    away = pl.BlockSpec(memory_space=pltpu.HBM)
    return pl.pallas_call(
        finish_kernel,
        out_shape=tuple(jax.ShapeDtypeStruct(g.shape, jnp.bfloat16) for g in grads),
        in_specs=[vmem] * 7,
        out_specs=(away,) * 3,
        scratch_shapes=[pltpu.VMEM(g.shape, jnp.bfloat16) for g in grads]
        + [pltpu.SemaphoreType.DMA((3 * TILES,))],
        compiler_params=pltpu.CompilerParams(vmem_limit_bytes=12 << 20),
        name="finish",
    )(*grads, rows, *hid)


def local(tokens, cotangent, expert_ids, gate_probs, gate_weight, up_weight, down_weight):
    groups = lax.axis_size("dp")
    window = lax.axis_size("win")
    mine = lax.axis_index("win")
    weights = (gate_weight[0], up_weight[0], down_weight[0])
    block = window * CAP

    def swap(value, axis, mask):
        pairs = [(i, i ^ mask) for i in range(lax.axis_size(axis))]
        return lax.ppermute(value, axis, pairs)

    def join(items):
        return jnp.concatenate(items, axis=0)

    rows, picker = front(
        mine.astype(jnp.int32)[None], expert_ids.T, gate_probs.T, tokens, cotangent, window
    )
    held = [rows[:CAP]]
    for index in range(1, window):
        held.append(swap(rows[index * CAP : (index + 1) * CAP], "win", index))

    rows = {0: join(held)}

    def pair(*masks):
        return join([rows[mask] for mask in masks])

    def bring(value, mask, *targets):
        received = swap(value, "slice", mask)
        for index, target in enumerate(targets):
            rows[target] = received[index * block : (index + 1) * block]

    bring(rows[0], 4, 4)
    bring(rows[0], 2, 2)
    bring(rows[0], 1, 1)
    bring(rows[4], 2, 6)
    bring(pair(2, 4), 1, 3, 5)
    bring(rows[6], 1, 7)

    hids, parts = {}, {}

    def turn(*masks):
        hid = hidden(pair(*masks), *weights)
        part = part_of(hid, *weights[:2])
        for index, mask in enumerate(masks):
            span = slice(index * block, (index + 1) * block)
            hids[mask] = [item[span] for item in hid]
            parts[mask] = part[span]

    def give(mask):
        value = join([parts[mask], parts[mask ^ 4]]).astype(jnp.bfloat16)
        return swap(value, "slice", mask)

    turn(0)
    turn(2, 4)
    back = lax.optimization_barrier(join([parts[0], parts[4]]))
    turn(6, 1)
    turn(3, 5, 7)
    incoming = [give(mask) for mask in (2, 3, 1)]
    last = parts[7]
    for part in incoming:
        back = back + part.astype(jnp.float32)

    far = swap(back[block:].astype(jnp.bfloat16), "slice", FAR)
    back = (back[:block] + far.astype(jnp.float32)).astype(jnp.bfloat16)
    kept = [back[:CAP]]
    for index in range(1, window):
        kept.append(swap(back[index * CAP : (index + 1) * CAP], "win", index))
    grad_input = lax.dot_general(
        picker, join(kept), TN, preferred_element_type=jnp.float32
    ).astype(jnp.bfloat16)

    order = list(rows)
    hid = [join(items) for items in zip(*(hids[index] for index in order))]
    grads = weight_grads(pair(*order), hid)
    grads = lax.optimization_barrier(grads)
    for mask in range(1, groups):
        pieces = [rows[0], pair(2, 4), pair(1, 6), pair(3, 5, 7)]
        if mask > 1:
            pieces, grads = lax.optimization_barrier((pieces, grads))
        theirs = [swap(piece, "dp", mask) for piece in pieces]
        early, _ = lax.optimization_barrier((theirs[:-1], last))
        early = join(early)
        more = weight_grads(early, hidden(early, *weights))
        grads = tuple(a + b for a, b in zip(grads, more))
        late = theirs[-1]
        hid = hidden(late, *weights)
        if mask < groups - 1:
            more = weight_grads(late, hid)
            grads = tuple(a + b for a, b in zip(grads, more))
        else:
            grads = finish(grads, late, hid)
    return (grad_input,) + tuple(g[None] for g in grads)


def solution(mesh):
    groups, devices = mesh.shape["dp"], mesh.shape["expert"]
    shape = (groups, SLICES, devices // SLICES)
    fine = Mesh(mesh.devices.reshape(shape), ("dp", "slice", "win"))
    rows = P(("dp", "slice", "win"), None)
    weight = P(("slice", "win"), None, None)
    return jax.shard_map(
        local,
        mesh=fine,
        in_specs=(rows, rows, rows, rows, weight, weight, weight),
        out_specs=(rows, weight, weight, weight),
        check_vma=False,
    )
```

```python
import functools

import jax
import jax.numpy as jnp
from jax import lax
from jax.experimental import pallas as pl
from jax.experimental.pallas import tpu as pltpu
from jax.sharding import Mesh, PartitionSpec as P


SLICES = 8
CAP = 8
FAR = 4


FRONT_VMEM = 55000 << 10
CHUNKS = 4

NT = (((1,), (1,)), ((), ()))
TN = (((0,), (0,)), ((), ()))


def silu_parts(gate_pre):
    sigmoid_value = jax.nn.sigmoid(gate_pre)
    return (gate_pre * sigmoid_value, sigmoid_value * (1.0 + gate_pre * (1.0 - sigmoid_value)))


def hidden(rows, gate_rows, up_rows, down_rows):
    width = gate_rows.shape[0]
    rows_in, rows_cot = rows[:, :width], rows[:, width:]
    gate_pre = jnp.dot(rows_in, gate_rows, preferred_element_type=jnp.float32)
    upward = jnp.dot(rows_in, up_rows, preferred_element_type=jnp.float32)
    dhidden = lax.dot_general(rows_cot, down_rows, NT, preferred_element_type=jnp.float32)
    swish, slope = silu_parts(gate_pre)
    active = (swish * upward).astype(jnp.bfloat16)
    dgate = (dhidden * upward * slope).astype(jnp.bfloat16)
    dupward = (dhidden * swish).astype(jnp.bfloat16)
    return active, dgate, dupward


def part_of(hid, gate_rows, up_rows):
    value = lax.dot_general(hid[1], gate_rows, NT, preferred_element_type=jnp.float32)
    return value + lax.dot_general(hid[2], up_rows, NT, preferred_element_type=jnp.float32)


def weight_grads(rows, hid):
    active, dgate, dupward = hid
    width = rows.shape[1] // 2
    rows_in, rows_cot = rows[:, :width], rows[:, width:]
    return (
        lax.dot_general(rows_in, dgate, TN, preferred_element_type=jnp.float32),
        lax.dot_general(rows_in, dupward, TN, preferred_element_type=jnp.float32),
        lax.dot_general(active, rows_cot, TN, preferred_element_type=jnp.float32),
    )


def front_kernel(window, mine_ref, ids_hbm, probs_hbm, tokens_hbm, cot_hbm, rows_ref, picker_ref,
                 ids_ref, probs_ref, tokens_ref, cot_ref, sems):
    copies = [
        pltpu.make_async_copy(ids_hbm, ids_ref, sems.at[0]),
        pltpu.make_async_copy(probs_hbm, probs_ref, sems.at[1]),
    ]
    size = tokens_ref.shape[0] // CHUNKS
    for source, target in ((tokens_hbm, tokens_ref), (cot_hbm, cot_ref)):
        for index in range(CHUNKS):
            part = pl.ds(index * size, size)
            copies.append(
                pltpu.make_async_copy(source.at[part], target.at[part], sems.at[len(copies)])
            )
    for copy in copies:
        copy.start()
    mine = mine_ref[0]
    count, width = tokens_ref.shape
    slots = window * CAP
    slot = lax.broadcasted_iota(jnp.int32, (slots, count), 0)
    earlier = lax.broadcasted_iota(jnp.int32, (count, count), 0) < lax.broadcasted_iota(
        jnp.int32, (count, count), 1
    )
    copies[0].wait()
    copies[1].wait()
    ids = ids_ref[...]
    probs = probs_ref[...]
    hit = jnp.zeros((slots, count), jnp.float32)
    chosen = jnp.zeros((slots, count), jnp.float32)
    for index in range(window):
        match = ids == (mine ^ index)
        hits = jnp.sum(match.astype(jnp.float32), axis=0, keepdims=True)
        prob = jnp.sum(jnp.where(match, probs, 0.0), axis=0, keepdims=True)
        here = slot // CAP == index
        hit = jnp.where(here, hits, hit)
        chosen = jnp.where(here, prob, chosen)
    rank = jnp.dot(
        hit.astype(jnp.bfloat16), earlier.astype(jnp.bfloat16), preferred_element_type=jnp.float32
    )
    placed = (hit == 1.0) & (rank.astype(jnp.int32) == slot % CAP)
    picker = placed.astype(jnp.bfloat16)
    picker_ref[...] = picker
    prob = jnp.sum(jnp.where(placed, chosen, 0.0), axis=1, keepdims=True)
    for copy in copies[2 : 2 + CHUNKS]:
        copy.wait()
    rows_in = jnp.dot(picker, tokens_ref[...], preferred_element_type=jnp.float32)
    rows_ref[:, :width] = rows_in.astype(jnp.bfloat16)
    for copy in copies[2 + CHUNKS :]:
        copy.wait()
    rows_cot = jnp.dot(picker, cot_ref[...], preferred_element_type=jnp.float32)
    rows_ref[:, width:] = (prob * rows_cot).astype(jnp.bfloat16)


def front(mine, ids, probs, tokens, cotangent, window):
    count, width = tokens.shape
    slots = window * CAP
    vmem = pl.BlockSpec(memory_space=pltpu.VMEM)
    away = pl.BlockSpec(memory_space=pltpu.HBM)
    return pl.pallas_call(
        functools.partial(front_kernel, window),
        out_shape=(
            jax.ShapeDtypeStruct((slots, 2 * width), jnp.bfloat16),
            jax.ShapeDtypeStruct((slots, count), jnp.bfloat16),
        ),
        in_specs=[pl.BlockSpec(memory_space=pltpu.SMEM), away, away, away, away],
        out_specs=(vmem, vmem),
        scratch_shapes=[
            pltpu.VMEM(ids.shape, ids.dtype),
            pltpu.VMEM(probs.shape, probs.dtype),
            pltpu.VMEM(tokens.shape, tokens.dtype),
            pltpu.VMEM(cotangent.shape, cotangent.dtype),
            pltpu.SemaphoreType.DMA((2 + 2 * CHUNKS,)),
        ],
        compiler_params=pltpu.CompilerParams(vmem_limit_bytes=FRONT_VMEM),
        name="front",
    )(mine, ids, probs, tokens, cotangent)


TILES = 8


def finish_kernel(gate_ref, up_ref, down_ref, rows_ref, active_ref, dgate_ref, dupward_ref,
                  gate_hbm, up_hbm, down_hbm, gate_out, up_out, down_out, sems):
    width = gate_ref.shape[0]
    tile = width // TILES
    copies = []

    def send(source, target, index):
        copy = pltpu.make_async_copy(source, target, sems.at[index])
        copy.start()
        copies.append(copy)

    units = dgate_ref.shape[1]
    slopes = jnp.concatenate([dgate_ref[...], dupward_ref[...]], axis=1)
    for index in range(TILES):
        part = pl.ds(index * tile, tile)
        rows_in = rows_ref[:, index * tile : (index + 1) * tile]
        rows_cot = rows_ref[:, width + index * tile : width + (index + 1) * tile]
        both = lax.dot_general(rows_in, slopes, TN, preferred_element_type=jnp.float32)
        for source, more, out, hbm, sem in (
            (gate_ref, both[:, :units], gate_out, gate_hbm, 0),
            (up_ref, both[:, units:], up_out, up_hbm, 1),
        ):
            out[part, :] = (source[part, :] + more).astype(jnp.bfloat16)
            send(out.at[part, :], hbm.at[part, :], 3 * index + sem)
        more = lax.dot_general(active_ref[...], rows_cot, TN, preferred_element_type=jnp.float32)
        down_out[:, part] = (down_ref[:, part] + more).astype(jnp.bfloat16)
        send(down_out.at[:, part], down_hbm.at[:, part], 3 * index + 2)
    for copy in copies:
        copy.wait()


def finish(grads, rows, hid):
    vmem = pl.BlockSpec(memory_space=pltpu.VMEM)
    away = pl.BlockSpec(memory_space=pltpu.HBM)
    return pl.pallas_call(
        finish_kernel,
        out_shape=tuple(jax.ShapeDtypeStruct(g.shape, jnp.bfloat16) for g in grads),
        in_specs=[vmem] * 7,
        out_specs=(away,) * 3,
        scratch_shapes=[pltpu.VMEM(g.shape, jnp.bfloat16) for g in grads]
        + [pltpu.SemaphoreType.DMA((3 * TILES,))],
        compiler_params=pltpu.CompilerParams(vmem_limit_bytes=12 << 20),
        name="finish",
    )(*grads, rows, *hid)


def local(tokens, cotangent, expert_ids, gate_probs, gate_weight, up_weight, down_weight):
    groups = lax.axis_size("dp")
    window = lax.axis_size("win")
    mine = lax.axis_index("win")
    weights = (gate_weight[0], up_weight[0], down_weight[0])
    block = window * CAP

    def swap(value, axis, mask):
        pairs = [(i, i ^ mask) for i in range(lax.axis_size(axis))]
        return lax.ppermute(value, axis, pairs)

    def join(items):
        return jnp.concatenate(items, axis=0)

    rows, picker = front(
        mine.astype(jnp.int32)[None],
        pltpu.with_memory_space_constraint(expert_ids.T, pltpu.HBM),
        pltpu.with_memory_space_constraint(gate_probs.T, pltpu.HBM),
        tokens, cotangent, window
    )
    split = [rows[index * CAP : (index + 1) * CAP] for index in range(window)]
    near = [split[0]]
    for index in range(1, window):
        near.append(swap(split[index], "win", index))
    far = []
    for index in range(window):
        pairs = []
        for s in range(SLICES):
            for e in range(window):
                pairs.append((s * window + e, (s ^ FAR) * window + (e ^ index)))
        far.append(lax.ppermute(split[index], ("slice", "win"), pairs))

    rows = {0: join(near), FAR: join(far)}

    def pair(*masks):
        return join([rows[mask] for mask in masks])

    def bring(value, mask, *targets):
        received = swap(value, "slice", mask)
        for index, target in enumerate(targets):
            rows[target] = received[index * block : (index + 1) * block]

    bring(rows[0], 2, 2)
    bring(rows[0], 1, 1)
    bring(rows[4], 2, 6)
    bring(pair(2, 4), 1, 3, 5)
    bring(rows[6], 1, 7)

    hids, parts = {}, {}

    def turn(*masks):
        hid = hidden(pair(*masks), *weights)
        part = part_of(hid, *weights[:2])
        for index, mask in enumerate(masks):
            span = slice(index * block, (index + 1) * block)
            hids[mask] = [item[span] for item in hid]
            parts[mask] = part[span]

    def give(mask):
        value = join([parts[mask], parts[mask ^ 4]]).astype(jnp.bfloat16)
        return swap(value, "slice", mask)

    turn(0)
    turn(2, 4)
    back = lax.optimization_barrier(join([parts[0], parts[4]]))
    turn(6, 1)
    turn(3, 5, 7)
    incoming = [give(mask) for mask in (2, 3, 1)]
    last = parts[7]
    for part in incoming:
        back = back + part.astype(jnp.float32)

    far = swap(back[block:].astype(jnp.bfloat16), "slice", FAR)
    back = (back[:block] + far.astype(jnp.float32)).astype(jnp.bfloat16)
    kept = [back[:CAP]]
    for index in range(1, window):
        kept.append(swap(back[index * CAP : (index + 1) * CAP], "win", index))
    grad_input = lax.dot_general(
        picker, join(kept), TN, preferred_element_type=jnp.float32
    ).astype(jnp.bfloat16)

    order = list(rows)
    hid = [join(items) for items in zip(*(hids[index] for index in order))]
    base, grads = pair(*order), None
    for mask in range(1, groups):
        pieces = [rows[0], pair(2, 4), pair(1, 6), pair(3, 5, 7)]
        if mask > 1:
            pieces, grads = lax.optimization_barrier((pieces, grads))
        theirs = [swap(piece, "dp", mask) for piece in pieces]
        early, _ = lax.optimization_barrier((theirs[:-1], last))
        early = join(early)
        more = hidden(early, *weights)
        if grads is None:
            early = join([base, early])
            more = [join(items) for items in zip(hid, more)]
        more = weight_grads(early, more)
        grads = more if grads is None else tuple(a + b for a, b in zip(grads, more))
        late = theirs[-1]
        more = hidden(late, *weights)
        if mask < groups - 1:
            more = weight_grads(late, more)
            grads = tuple(a + b for a, b in zip(grads, more))
        if mask == groups - 1:
            grads = finish(grads, late, more)
    return (grad_input,) + tuple(g[None] for g in grads)


def solution(mesh):
    groups, devices = mesh.shape["dp"], mesh.shape["expert"]
    shape = (groups, SLICES, devices // SLICES)
    fine = Mesh(mesh.devices.reshape(shape), ("dp", "slice", "win"))
    rows = P(("dp", "slice", "win"), None)
    weight = P(("slice", "win"), None, None)
    return jax.shard_map(
        local,
        mesh=fine,
        in_specs=(rows, rows, rows, rows, weight, weight, weight),
        out_specs=(rows, weight, weight, weight),
        check_vma=False,
    )
```

```python
import functools

import jax
import jax.numpy as jnp
from jax import lax
from jax.experimental import pallas as pl
from jax.experimental.pallas import tpu as pltpu
from jax.sharding import Mesh, PartitionSpec as P


SLICES = 8
CAP = 8
FAR = 4


FRONT_VMEM = 55000 << 10
CHUNKS = 1

NT = (((1,), (1,)), ((), ()))
TN = (((0,), (0,)), ((), ()))


def silu_parts(gate_pre):
    sigmoid_value = jax.nn.sigmoid(gate_pre)
    return (gate_pre * sigmoid_value, sigmoid_value * (1.0 + gate_pre * (1.0 - sigmoid_value)))


def hidden(rows, gate_rows, up_rows, down_rows):
    width = gate_rows.shape[0]
    rows_in, rows_cot = rows[:, :width], rows[:, width:]
    gate_pre = jnp.dot(rows_in, gate_rows, preferred_element_type=jnp.float32)
    upward = jnp.dot(rows_in, up_rows, preferred_element_type=jnp.float32)
    dhidden = lax.dot_general(rows_cot, down_rows, NT, preferred_element_type=jnp.float32)
    swish, slope = silu_parts(gate_pre)
    active = (swish * upward).astype(jnp.bfloat16)
    dgate = (dhidden * upward * slope).astype(jnp.bfloat16)
    dupward = (dhidden * swish).astype(jnp.bfloat16)
    return active, dgate, dupward


def part_of(hid, gate_rows, up_rows):
    value = lax.dot_general(hid[1], gate_rows, NT, preferred_element_type=jnp.float32)
    return value + lax.dot_general(hid[2], up_rows, NT, preferred_element_type=jnp.float32)


def weight_grads(rows, hid):
    active, dgate, dupward = hid
    width = rows.shape[1] // 2
    rows_in, rows_cot = rows[:, :width], rows[:, width:]
    return (
        lax.dot_general(rows_in, dgate, TN, preferred_element_type=jnp.float32),
        lax.dot_general(rows_in, dupward, TN, preferred_element_type=jnp.float32),
        lax.dot_general(active, rows_cot, TN, preferred_element_type=jnp.float32),
    )


def front_kernel(window, mine_ref, ids_hbm, probs_hbm, tokens_hbm, cot_hbm, rows_ref, picker_ref,
                 ids_ref, probs_ref, tokens_ref, cot_ref, sems):
    copies = [
        pltpu.make_async_copy(ids_hbm, ids_ref, sems.at[0]),
        pltpu.make_async_copy(probs_hbm, probs_ref, sems.at[1]),
    ]
    size = tokens_ref.shape[0] // CHUNKS
    for source, target in ((tokens_hbm, tokens_ref), (cot_hbm, cot_ref)):
        for index in range(CHUNKS):
            part = pl.ds(index * size, size)
            copies.append(
                pltpu.make_async_copy(source.at[part], target.at[part], sems.at[len(copies)])
            )
    for copy in copies:
        copy.start()
    mine = mine_ref[0]
    count, width = tokens_ref.shape
    slots = window * CAP
    slot = lax.broadcasted_iota(jnp.int32, (slots, count), 0)
    earlier = lax.broadcasted_iota(jnp.int32, (count, count), 0) < lax.broadcasted_iota(
        jnp.int32, (count, count), 1
    )
    copies[0].wait()
    copies[1].wait()
    ids = ids_ref[...]
    probs = probs_ref[...]
    hit = jnp.zeros((slots, count), jnp.float32)
    chosen = jnp.zeros((slots, count), jnp.float32)
    for index in range(window):
        match = ids == (mine ^ index)
        hits = jnp.sum(match.astype(jnp.float32), axis=0, keepdims=True)
        prob = jnp.sum(jnp.where(match, probs, 0.0), axis=0, keepdims=True)
        here = slot // CAP == index
        hit = jnp.where(here, hits, hit)
        chosen = jnp.where(here, prob, chosen)
    rank = jnp.dot(
        hit.astype(jnp.bfloat16), earlier.astype(jnp.bfloat16), preferred_element_type=jnp.float32
    )
    placed = (hit == 1.0) & (rank.astype(jnp.int32) == slot % CAP)
    picker = placed.astype(jnp.bfloat16)
    picker_ref[...] = picker
    prob = jnp.sum(jnp.where(placed, chosen, 0.0), axis=1, keepdims=True)
    for copy in copies[2 : 2 + CHUNKS]:
        copy.wait()
    rows_in = jnp.dot(picker, tokens_ref[...], preferred_element_type=jnp.float32)
    rows_ref[:, :width] = rows_in.astype(jnp.bfloat16)
    for copy in copies[2 + CHUNKS :]:
        copy.wait()
    rows_cot = jnp.dot(picker, cot_ref[...], preferred_element_type=jnp.float32)
    rows_ref[:, width:] = (prob * rows_cot).astype(jnp.bfloat16)


def front(mine, ids, probs, tokens, cotangent, window):
    count, width = tokens.shape
    slots = window * CAP
    vmem = pl.BlockSpec(memory_space=pltpu.VMEM)
    away = pl.BlockSpec(memory_space=pltpu.HBM)
    return pl.pallas_call(
        functools.partial(front_kernel, window),
        out_shape=(
            jax.ShapeDtypeStruct((slots, 2 * width), jnp.bfloat16),
            jax.ShapeDtypeStruct((slots, count), jnp.bfloat16),
        ),
        in_specs=[pl.BlockSpec(memory_space=pltpu.SMEM), away, away, away, away],
        out_specs=(vmem, vmem),
        scratch_shapes=[
            pltpu.VMEM(ids.shape, ids.dtype),
            pltpu.VMEM(probs.shape, probs.dtype),
            pltpu.VMEM(tokens.shape, tokens.dtype),
            pltpu.VMEM(cotangent.shape, cotangent.dtype),
            pltpu.SemaphoreType.DMA((2 + 2 * CHUNKS,)),
        ],
        compiler_params=pltpu.CompilerParams(vmem_limit_bytes=FRONT_VMEM),
        name="front",
    )(mine, ids, probs, tokens, cotangent)


TILES = 8


def finish_kernel(gate_ref, up_ref, down_ref, rows_ref, active_ref, dgate_ref, dupward_ref,
                  gate_hbm, up_hbm, down_hbm, gate_out, up_out, down_out, sems):
    width = gate_ref.shape[0]
    tile = width // TILES
    copies = []

    def send(source, target, index):
        copy = pltpu.make_async_copy(source, target, sems.at[index])
        copy.start()
        copies.append(copy)

    units = dgate_ref.shape[1]
    slopes = jnp.concatenate([dgate_ref[...], dupward_ref[...]], axis=1)
    for index in range(TILES):
        part = pl.ds(index * tile, tile)
        rows_in = rows_ref[:, index * tile : (index + 1) * tile]
        rows_cot = rows_ref[:, width + index * tile : width + (index + 1) * tile]
        both = lax.dot_general(rows_in, slopes, TN, preferred_element_type=jnp.float32)
        for source, more, out, hbm, sem in (
            (gate_ref, both[:, :units], gate_out, gate_hbm, 0),
            (up_ref, both[:, units:], up_out, up_hbm, 1),
        ):
            out[part, :] = (source[part, :] + more).astype(jnp.bfloat16)
            send(out.at[part, :], hbm.at[part, :], 3 * index + sem)
        more = lax.dot_general(active_ref[...], rows_cot, TN, preferred_element_type=jnp.float32)
        down_out[:, part] = (down_ref[:, part] + more).astype(jnp.bfloat16)
        send(down_out.at[:, part], down_hbm.at[:, part], 3 * index + 2)
    for copy in copies:
        copy.wait()


def finish(grads, rows, hid):
    vmem = pl.BlockSpec(memory_space=pltpu.VMEM)
    away = pl.BlockSpec(memory_space=pltpu.HBM)
    return pl.pallas_call(
        finish_kernel,
        out_shape=tuple(jax.ShapeDtypeStruct(g.shape, jnp.bfloat16) for g in grads),
        in_specs=[vmem] * 7,
        out_specs=(away,) * 3,
        scratch_shapes=[pltpu.VMEM(g.shape, jnp.bfloat16) for g in grads]
        + [pltpu.SemaphoreType.DMA((3 * TILES,))],
        compiler_params=pltpu.CompilerParams(vmem_limit_bytes=12 << 20),
        name="finish",
    )(*grads, rows, *hid)


def local(tokens, cotangent, expert_ids, gate_probs, gate_weight, up_weight, down_weight):
    groups = lax.axis_size("dp")
    window = lax.axis_size("win")
    mine = lax.axis_index("win")
    weights = (gate_weight[0], up_weight[0], down_weight[0])
    block = window * CAP

    def swap(value, axis, mask):
        pairs = [(i, i ^ mask) for i in range(lax.axis_size(axis))]
        return lax.ppermute(value, axis, pairs)

    def join(items):
        return jnp.concatenate(items, axis=0)

    rows, picker = front(
        mine.astype(jnp.int32)[None],
        pltpu.with_memory_space_constraint(expert_ids.T, pltpu.HBM),
        pltpu.with_memory_space_constraint(gate_probs.T, pltpu.HBM),
        tokens, cotangent, window
    )

    def send_far(value, index):
        pairs = []
        for s in range(SLICES):
            for e in range(window):
                pairs.append((s * window + e, (s ^ FAR) * window + (e ^ index)))
        return lax.ppermute(value, ("slice", "win"), pairs)

    parcels = [rows[index * CAP : (index + 1) * CAP] for index in range(window)]
    near = [parcels[0]]
    for index in range(1, window):
        near.append(swap(parcels[index], "win", index))
    far = [send_far(item, index) for index, item in enumerate(parcels)]

    rows = {0: join(near), FAR: join(far)}

    def pair(*masks):
        return join([rows[mask] for mask in masks])

    def bring(value, mask, *targets):
        received = swap(value, "slice", mask)
        for index, target in enumerate(targets):
            rows[target] = received[index * block : (index + 1) * block]

    bring(rows[0], 2, 2)
    bring(rows[0], 1, 1)
    bring(rows[4], 2, 6)
    bring(pair(2, 4), 1, 3, 5)
    bring(rows[6], 1, 7)

    hids, parts = {}, {}

    def turn(*masks):
        hid = hidden(pair(*masks), *weights)
        part = part_of(hid, *weights[:2])
        for index, mask in enumerate(masks):
            span = slice(index * block, (index + 1) * block)
            hids[mask] = [item[span] for item in hid]
            parts[mask] = part[span]

    def give(mask):
        value = join([parts[mask], parts[mask ^ 4]]).astype(jnp.bfloat16)
        return swap(value, "slice", mask)

    turn(0)
    turn(2, 4)
    back = lax.optimization_barrier(join([parts[0], parts[4]]))
    turn(6, 1)
    turn(3, 5, 7)
    incoming = [give(mask) for mask in (2, 3)]
    halves = [swap(parts[mask].astype(jnp.bfloat16), "slice", 1) for mask in (1, 1 ^ FAR)]
    incoming.append(join(halves))
    last = parts[7]
    for part in incoming:
        back = back + part.astype(jnp.float32)

    def split(value):
        return [value[index * CAP : (index + 1) * CAP] for index in range(window)]

    here, there = split(back[:block]), split(back[block:].astype(jnp.bfloat16))
    kept = []
    for index in range(window):
        theirs = send_far(there[index], index)
        mine = here[index]
        if index:
            mine = swap(mine.astype(jnp.bfloat16), "win", index)
        kept.append((mine.astype(jnp.float32) + theirs.astype(jnp.float32)).astype(jnp.bfloat16))
    grad_input = lax.dot_general(
        picker, join(kept), TN, preferred_element_type=jnp.float32
    ).astype(jnp.bfloat16)

    order = list(rows)
    hid = [join(items) for items in zip(*(hids[index] for index in order))]
    base, grads = pair(*order), None
    for mask in range(1, groups):
        pieces = [rows[0], pair(2, 4), pair(1, 6), pair(3, 5, 7)]
        if mask > 1:
            pieces, grads = lax.optimization_barrier((pieces, grads))
        theirs = [swap(piece, "dp", mask) for piece in pieces]
        early, _ = lax.optimization_barrier((theirs[:-1], last))
        early = join(early)
        more = hidden(early, *weights)
        if grads is None:
            early = join([base, early])
            more = [join(items) for items in zip(hid, more)]
        more = weight_grads(early, more)
        grads = more if grads is None else tuple(a + b for a, b in zip(grads, more))
        late = theirs[-1]
        more = hidden(late, *weights)
        if mask < groups - 1:
            more = weight_grads(late, more)
            grads = tuple(a + b for a, b in zip(grads, more))
        if mask == groups - 1:
            grads = finish(grads, late, more)
    return (grad_input,) + tuple(g[None] for g in grads)


def solution(mesh):
    groups, devices = mesh.shape["dp"], mesh.shape["expert"]
    shape = (groups, SLICES, devices // SLICES)
    fine = Mesh(mesh.devices.reshape(shape), ("dp", "slice", "win"))
    rows = P(("dp", "slice", "win"), None)
    weight = P(("slice", "win"), None, None)
    return jax.shard_map(
        local,
        mesh=fine,
        in_specs=(rows, rows, rows, rows, weight, weight, weight),
        out_specs=(rows, weight, weight, weight),
        check_vma=False,
    )
```
